32 devices in a mesh: src: 4 (over y, core), help: 8 (over z, x).
Axes of the slice: x: 2, y: 2, z: 4, core: 2. Of those that a mesh axis runs over, the one named last changes fastest.
Arguments:
- tiles: int32 [2, 256], P(None, 'src'), may hold values from 0 to 31, as said below
- cell_slot: int32 [2, 32], replicated, may hold values from 0 to 31, as said below
- counts: int32 [32, 2], P(('src', 'help')), may hold values from 128 to 512, as said below
- src_points: bfloat16 [16384, 512], P(('src', 'help')), may hold values from -9 to 9
- tgt_points: bfloat16 [16384, 512], P(('src', 'help')), may hold values from -9 to 9
Outputs:
- source_potential: float32 [16384], P(('src', 'help'))
- target_potential: float32 [16384], P(('src', 'help'))
- transport: float32 [16384, 512], P(('src', 'help'))
The draws below stay inside these ranges and needn't reach their ends.
Inputs may be any that keep to these rules, and one draw needn't show every extreme that they name: `tiles`: columns come in blocks of 64, block g for group g of 8 cells: a block's source cells have ids g * 8 to g * 8 + 7, its target cells lie in group g or in group g + 1 (group 4 - 1 is followed by group 0); no pair is listed twice, and every source cell and every target cell is named in some column. Each row is a permutation that keeps every cell in its group: cell c is stored at slot cell_slot[side, c], with cell_slot[side, c] // 8 equal to c // 8; slot k is rows k * 512 to k * 512 + 511 of the point arrays. `counts`: rows of a slot at and beyond its count are padding. Both ends of the range occur in each column.
All inputs are finite; a program needn't handle non-finite values.
Results may differ from the reference program's by a relative error of at most 0.004.
Values may be sent and summed in bfloat16 or wider, within the bound.
A program may use at most 192 MiB of HBM per device.

```python
import math
import jax
import jax.numpy as jnp
from jax import lax

D = 512
P_SIZE = 512
ITERS = 2
GROUP = 8
GROUPS = 4
NCELL = 32
TPG = 64
TILES = 256


def draw_tiles(key, part):

    def one_group(index):
        group_key = jax.random.fold_in(key, index + 11)
        pair_ids = jnp.arange(2 * GROUP * GROUP, dtype=jnp.int32)
        src_local = pair_ids // (2 * GROUP)
        tgt_local = pair_ids % (2 * GROUP)
        perm_own = jax.random.permutation(jax.random.fold_in(group_key, 4), GROUP)
        perm_next = jax.random.permutation(jax.random.fold_in(group_key, 5), GROUP)
        partner = jnp.where(tgt_local < GROUP, perm_own[tgt_local % GROUP], perm_next[tgt_local % GROUP])
        is_cover = src_local == partner
        ranking = jax.random.permutation(jax.random.fold_in(group_key, 1), GROUP)
        is_hot = ranking[src_local] < min(4, GROUP)
        jitter = jax.random.randint(jax.random.fold_in(group_key, 2), pair_ids.shape, 0, 1024, dtype=jnp.int32)
        scores = jnp.where(is_cover, 1 << 29, is_hot.astype(jnp.int32) * (1 << 21) + jitter * 1024) + pair_ids
        picked = lax.top_k(scores, TPG)[1]
        picked = picked[jax.random.permutation(jax.random.fold_in(group_key, 3), TPG)]
        src_ids = index * GROUP + src_local[picked]
        tgt_group = jnp.where(tgt_local[picked] < GROUP, index, (index + 1) % GROUPS)
        tgt_ids = tgt_group * GROUP + tgt_local[picked] % GROUP
        return jnp.stack([src_ids, tgt_ids])
    blocks = jax.vmap(one_group)(jnp.arange(GROUPS, dtype=jnp.int32))
    return jnp.transpose(blocks, (1, 0, 2)).reshape(2, TILES).astype(jnp.int32)


def draw_cell_slot(key, part):

    def one_block(index):
        shuffled = jax.random.permutation(jax.random.fold_in(key, index + 101), GROUP)
        return index % GROUPS * GROUP + shuffled
    slots = jax.vmap(one_block)(jnp.arange(2 * GROUPS, dtype=jnp.int32))
    return slots.reshape(2, NCELL).astype(jnp.int32)


def draw_counts(key, part):
    counted = jax.random.randint(jax.random.fold_in(key, 7), (NCELL, 2), P_SIZE // 4, P_SIZE + 1, dtype=jnp.int32)
    places = jax.random.randint(jax.random.fold_in(key, 8), (2,), 0, NCELL, dtype=jnp.int32)
    counted = counted.at[places[0], 0].set(P_SIZE).at[(places[0] + 1) % NCELL, 0].set(P_SIZE // 4)
    counted = counted.at[places[1], 1].set(P_SIZE).at[(places[1] + 1) % NCELL, 1].set(P_SIZE // 4)
    return counted


def point_cloud(key, salt, offset_on, cell_spread_on):
    base_key = jax.random.fold_in(key, salt)
    values = jax.random.normal(jax.random.fold_in(base_key, 1), (NCELL * P_SIZE, D), jnp.float32)
    if offset_on:
        strength_table = jnp.array([0.0, 0.0, 0.0, 7.0, 0.0, 9.0, 11.0, 0.0], jnp.float32)
        slot_ids = jnp.arange(NCELL, dtype=jnp.int32) % 8
        strength = strength_table[slot_ids]
        signs = (jax.random.randint(jax.random.fold_in(base_key, 3), (D,), 0, 2, dtype=jnp.int32) * 2 - 1).astype(jnp.float32)
        shift = strength[:, None, None] * signs[None, None, :] * float(D) ** (-0.25)
        values = (values.reshape(NCELL, P_SIZE, D) + shift).reshape(NCELL * P_SIZE, D)
    if cell_spread_on:
        cell_spread = jnp.exp(jax.random.uniform(jax.random.fold_in(base_key, 4), (NCELL, 1, 1), jnp.float32, math.log(0.6), math.log(3.0)))
        values = (values.reshape(NCELL, P_SIZE, D) * cell_spread).reshape(NCELL * P_SIZE, D)
    return jnp.clip(values, -9.0, 9.0).astype(jnp.bfloat16)


def draw_src_points(key, part):
    return point_cloud(key, 501, True, False)


def draw_tgt_points(key, part):
    return point_cloud(key, 502, False, True)


def setup_inputs(seed: int = 0) -> dict:
    seeds = jax.random.split(jax.random.key(seed), 6)
    tiles = draw_tiles(jax.random.fold_in(seeds[5], 71), 0)
    cell_slot = draw_cell_slot(jax.random.fold_in(seeds[5], 71), 0)
    counts = draw_counts(jax.random.fold_in(seeds[5], 71), 0)
    src_points = draw_src_points(jax.random.fold_in(seeds[5], 71), 0)
    tgt_points = draw_tgt_points(jax.random.fold_in(seeds[5], 71), 0)
    return {"tiles": tiles, "cell_slot": cell_slot, "counts": counts, "src_points": src_points, "tgt_points": tgt_points}


EPSILON = 0.2
NEGATIVE = -1e+30

def join_parts(first, second):
    highest = jnp.maximum(first[0], second[0])
    return (highest, first[1] * jnp.exp(first[0] - highest) + second[1] * jnp.exp(second[0] - highest))

def reference(tiles, cell_slot, counts, src_points, tgt_points):
    cost_scale = math.sqrt(D)
    source_cells = src_points.reshape(NCELL, P_SIZE, D)
    target_cells = tgt_points.reshape(NCELL, P_SIZE, D)
    source_half = 0.5 * lax.optimization_barrier(jnp.sum(jnp.square(source_cells.astype(jnp.float32)), axis=2))
    target_half = 0.5 * lax.optimization_barrier(jnp.sum(jnp.square(target_cells.astype(jnp.float32)), axis=2))
    positions = jnp.arange(P_SIZE, dtype=jnp.int32)
    source_live = positions[None, :] < counts[:, 0:1]
    target_live = positions[None, :] < counts[:, 1:2]
    source_slots = jnp.take(cell_slot[0], tiles[0]).astype(jnp.int32)
    target_slots = jnp.take(cell_slot[1], tiles[1]).astype(jnp.int32)
    pairs = (source_slots, target_slots)

    def tile_cost(src_cell, tgt_cell):
        inner = jnp.dot(source_cells[src_cell], target_cells[tgt_cell].T, preferred_element_type=jnp.float32)
        cost_tile = (source_half[src_cell][:, None] + target_half[tgt_cell][None, :] - inner) / cost_scale
        listed = source_live[src_cell][:, None] & target_live[tgt_cell][None, :]
        return (cost_tile, listed)

    def start_tables():
        return (jnp.full((NCELL, P_SIZE), NEGATIVE, jnp.float32), jnp.zeros((NCELL, P_SIZE), jnp.float32))

    def row_pass(target_potential):

        def visit(tables, pair):
            src_cell, tgt_cell = pair
            cost_tile, listed = tile_cost(src_cell, tgt_cell)
            scores = jnp.where(listed, (target_potential[tgt_cell][None, :] - cost_tile) / EPSILON, NEGATIVE)
            part_max = lax.optimization_barrier(jnp.max(scores, axis=1))
            part_sum = lax.optimization_barrier(jnp.sum(jnp.exp(scores - part_max[:, None]), axis=1))
            joined = join_parts((tables[0][src_cell], tables[1][src_cell]), (part_max, part_sum))
            return ((tables[0].at[src_cell].set(joined[0]), tables[1].at[src_cell].set(joined[1])), None)
        tables, unused = lax.scan(visit, start_tables(), pairs)
        return jnp.where(source_live, -EPSILON * (tables[0] + jnp.log(tables[1])), 0.0)

    def col_pass(source_potential):

        def visit(tables, pair):
            src_cell, tgt_cell = pair
            cost_tile, listed = tile_cost(src_cell, tgt_cell)
            scores = jnp.where(listed, (source_potential[src_cell][:, None] - cost_tile) / EPSILON, NEGATIVE)
            part_max = lax.optimization_barrier(jnp.max(scores, axis=0))
            part_sum = lax.optimization_barrier(jnp.sum(jnp.exp(scores - part_max[None, :]), axis=0))
            joined = join_parts((tables[0][tgt_cell], tables[1][tgt_cell]), (part_max, part_sum))
            return ((tables[0].at[tgt_cell].set(joined[0]), tables[1].at[tgt_cell].set(joined[1])), None)
        tables, unused = lax.scan(visit, start_tables(), pairs)
        return jnp.where(target_live, -EPSILON * (tables[0] + jnp.log(tables[1])), 0.0)
    target_potential = jnp.zeros((NCELL, P_SIZE), jnp.float32)
    source_potential = jnp.zeros((NCELL, P_SIZE), jnp.float32)
    for sweep in range(ITERS):
        source_potential = row_pass(target_potential)
        target_potential = col_pass(source_potential)

    def accumulate(sums, pair):
        src_cell, tgt_cell = pair
        cost_tile, listed = tile_cost(src_cell, tgt_cell)
        exponent = (source_potential[src_cell][:, None] + target_potential[tgt_cell][None, :] - cost_tile) / EPSILON
        weight = jnp.where(listed, jnp.exp(exponent), 0.0).astype(jnp.bfloat16)
        numerator = sums[0].at[src_cell].add(jnp.dot(weight, target_cells[tgt_cell], preferred_element_type=jnp.float32))
        denominator = sums[1].at[src_cell].add(lax.optimization_barrier(jnp.sum(weight.astype(jnp.float32), axis=1)))
        return ((numerator, denominator), None)
    start = (jnp.zeros((NCELL, P_SIZE, D), jnp.float32), jnp.zeros((NCELL, P_SIZE), jnp.float32))
    sums, unused = lax.scan(accumulate, start, pairs)
    safe_total = jnp.where(source_live, sums[1], 1.0)
    transport = jnp.where(source_live[:, :, None], sums[0] / safe_total[:, :, None], 0.0)
    return (source_potential.reshape(NCELL * P_SIZE), target_potential.reshape(NCELL * P_SIZE), transport.reshape(NCELL * P_SIZE, D))
```

```python
import functools
import math

import jax
import jax.numpy as jnp
from jax import lax
from jax.experimental import pallas as pl
from jax.experimental.pallas import tpu as pltpu
from jax.sharding import PartitionSpec as P

ITERS = 2
EPSILON = 0.2
NEGATIVE = -1e30
LANES = 128
MESH = pl.DeviceIdType.MESH


def line_length(count):
    return 1 << ((count.bit_length()) // 2)


def lookup(cell_ids, slot_table):
    matches = cell_ids[:, None] == jnp.arange(slot_table.shape[0], dtype=jnp.int32)[None, :]
    return jnp.sum(jnp.where(matches, slot_table[None, :], 0), axis=1)


def kernel(
    groups, n, zs, xs, scale,
    src_ref, tgt_ref, aux_ref, tlive_ref, slive_ref, listed_ref,
    num_ref, den_ref, f_ref, g_ref,
    pts, aux, inner, peak, total, part, inbox, gbuf,
    local_sem, rp, ra, sp, sa, part_send, part_recv, g_send, g_recv,
):
    s = lax.axis_index("src")
    h = lax.axis_index("help")
    z, x = h // xs, h % xs
    nxt = (s + 1) % groups
    prv = (s + groups - 1) % groups
    rows, width = src_ref.shape
    quarters = rows // LANES

    cp = pltpu.make_async_copy(tgt_ref, pts.at[0, h], local_sem.at[0])
    ca = pltpu.make_async_copy(aux_ref, aux.at[0, h], local_sem.at[1])
    cp.start()
    ca.start()

    barrier = pltpu.get_barrier_semaphore()

    @pl.loop(0, n)
    def _(k):
        pl.semaphore_signal(barrier, inc=1, device_id={"src": nxt, "help": k}, device_id_type=MESH)
        pl.semaphore_signal(barrier, inc=1, device_id={"src": prv, "help": k}, device_id_type=MESH)

        @pl.when(k != h)
        def _():
            pl.semaphore_signal(barrier, inc=1, device_id={"src": s, "help": k}, device_id_type=MESH)

    peak[...] = jnp.full_like(peak, NEGATIVE)
    total[...] = jnp.zeros_like(total)
    den_ref[...] = jnp.zeros_like(den_ref)
    num_ref[...] = jnp.zeros_like(num_ref)

    def row_update(index, g):
        chunk = 32

        @pl.loop(0, rows // chunk, unroll=2)
        def _(r):
            at = pl.ds(pl.multiple_of(r * chunk, chunk), chunk)
            old = peak[at, :]
            vals = [
                inner[index, at, q * LANES:(q + 1) * LANES] + g[:, q * LANES:(q + 1) * LANES]
                for q in range(quarters)
            ]
            new = functools.reduce(jnp.maximum, vals, old)
            acc = total[at, :] * jnp.exp2(old - new)
            for v in vals:
                acc = acc + jnp.exp2(v - new)
            peak[at, :] = new
            total[at, :] = acc

    def row_finish():
        chunk = 64

        @pl.loop(0, rows // chunk)
        def _(r):
            at = pl.ds(pl.multiple_of(r * chunk, chunk), chunk)
            m = jnp.max(peak[at, :], axis=1, keepdims=True)
            t = jnp.sum(total[at, :] * jnp.exp2(peak[at, :] - m), axis=1, keepdims=True)
            f = -(m + jnp.log2(t))
            f_ref[at, :] = jnp.where(slive_ref[at, :] > 0, f, NEGATIVE)

    def block(side, slot):
        index = side * n + slot
        inner[index] = scale * lax.dot_general(
            src_ref[...], pts[side, slot], (((1,), (1,)), ((), ())),
            preferred_element_type=jnp.float32,
        )
        row_update(index, aux[side, slot] + listed_ref[index])

    def moves(kind, slot, side, dev):
        return (
            pltpu.make_async_remote_copy(
                src_ref=pts.at[0, slot], dst_ref=pts.at[side, slot],
                send_sem=sp.at[kind, slot], recv_sem=rp.at[side, slot],
                device_id=dev, device_id_type=MESH),
            pltpu.make_async_remote_copy(
                src_ref=aux.at[0, slot], dst_ref=aux.at[side, slot],
                send_sem=sa.at[kind, slot], recv_sem=ra.at[side, slot],
                device_id=dev, device_id_type=MESH),
        )

    def await_cell(side, slot):
        pltpu.make_async_copy(pts.at[side, slot], pts.at[side, slot], rp.at[side, slot]).wait()
        pltpu.make_async_copy(aux.at[side, slot], aux.at[side, slot], ra.at[side, slot]).wait()

    def each_move(slot, act):
        zz, xx = slot // xs, slot % xs
        mine = xx == x

        @pl.when(mine & (zz <= z) & (z + 1 < zs))
        def _():
            act(moves(0, slot, 0, {"src": s, "help": h + xs}))

        @pl.when(mine & (zz >= z) & (z >= 1))
        def _():
            act(moves(1, slot, 0, {"src": s, "help": h - xs}))

        for k in range(1, xs):
            @pl.when(mine)
            def _(k=k):
                act(moves(2 + k, slot, 0, {"src": s, "help": z * xs + (x + k) % xs}))

        act(moves(2, slot, 1, {"src": prv, "help": h}))

    def start(pair):
        for c in pair:
            c.start()

    def finish(pair):
        for c in pair:
            c.wait_send()

    cp.wait()
    ca.wait()
    pl.semaphore_wait(barrier, 3 * n - 1)

    def entry(e, dist):
        xoff = (e // 2) % xs
        low = e % 2
        far = dist - jnp.where(xoff > 0, 1, 0)
        zz = jnp.where(low == 0, z - far, z + far)
        valid = (far >= 0) & (far < zs) & (zz >= 0) & (zz < zs) & ((far > 0) | (low == 0))
        return valid, jnp.clip(zz, 0, zs - 1) * xs + (x + xoff) % xs

    @pl.loop(0, zs + 3)
    def _(d):
        @pl.loop(0, 2 * xs)
        def _(e):
            valid, slot = entry(e, d)

            @pl.when(valid)
            def _():
                @pl.when(slot != h)
                def _():
                    await_cell(0, slot)

                each_move(slot, start)

        @pl.loop(0, 4 * xs)
        def _(e):
            side = e // (2 * xs)
            valid, slot = entry(e % (2 * xs), d - 2 * side)

            @pl.when(valid)
            def _():
                @pl.when(side == 1)
                def _():
                    await_cell(1, slot)

                block(side, slot)

    def column(index):
        chunk = 64

        def step(r, state):
            m, t = state
            at = pl.ds(pl.multiple_of(r * chunk, chunk), chunk)
            f = f_ref[at, :]
            v = inner[index, at, :] + jnp.concatenate([f] * quarters, axis=1)
            v = v.reshape(chunk // 8, 8, rows)
            new = jnp.maximum(m, jnp.max(v, axis=0))
            t = t * jnp.exp2(m - new) + jnp.sum(jnp.exp2(v - new[None]), axis=0)
            return new, t

        m, t = lax.fori_loop(
            0, rows // chunk, step,
            (jnp.full((8, rows), NEGATIVE, jnp.float32), jnp.zeros((8, rows), jnp.float32)),
        )
        top = jnp.max(m, axis=0, keepdims=True)
        t = jnp.sum(t * jnp.exp2(m - top), axis=0, keepdims=True)
        return top + listed_ref[index], t

    for sweep in range(ITERS):
        row_finish()

        def part_move(side, slot):
            return pltpu.make_async_remote_copy(
                src_ref=part.at[sweep, side, slot], dst_ref=inbox.at[sweep, side, h],
                send_sem=part_send.at[sweep, side, slot], recv_sem=part_recv.at[sweep, side, h],
                device_id={"src": jnp.where(side == 0, s, nxt), "help": slot}, device_id_type=MESH)

        def g_move(side, k):
            return pltpu.make_async_remote_copy(
                src_ref=gbuf.at[sweep, 0, h], dst_ref=gbuf.at[sweep, side, h],
                send_sem=g_send.at[sweep, side, k], recv_sem=g_recv.at[sweep, side, h],
                device_id={"src": jnp.where(side == 0, s, prv), "help": k}, device_id_type=MESH)

        @pl.loop(0, 2 * n)
        def _(e):
            side = 1 - e // n
            slot = (h + 1 + e) % n
            top, t = column(side * n + slot)
            part[sweep, side, slot, 0:1, :] = top
            part[sweep, side, slot, 1:2, :] = t

            @pl.when((side == 1) | (slot != h))
            def _():
                part_move(side, slot).start()

        def join(e, state):
            m, t = state
            side, k = e // n, e % n
            m2 = inbox[sweep, side, k, 0:1, :]
            t2 = inbox[sweep, side, k, 1:2, :]
            new = jnp.maximum(m, m2)
            return new, t * jnp.exp2(m - new) + t2 * jnp.exp2(m2 - new)

        @pl.loop(0, 2 * n)
        def _(e):
            side, k = e // n, e % n

            @pl.when((side == 1) | (k != h))
            def _():
                pltpu.make_async_copy(
                    inbox.at[sweep, side, k], inbox.at[sweep, side, k],
                    part_recv.at[sweep, side, k]).wait()

        inbox[sweep, 0, h] = part[sweep, 0, h]
        m, t = lax.fori_loop(
            1, 2 * n, join, (inbox[sweep, 0, 0, 0:1, :], inbox[sweep, 0, 0, 1:2, :]), unroll=True)
        g = jnp.where(tlive_ref[...] > 0, -(m + jnp.log2(t)), NEGATIVE)
        gbuf[sweep, 0, h] = g
        g_ref[...] = g

        @pl.loop(0, 2 * n)
        def _(e):
            side, k = e // n, e % n

            @pl.when((side == 1) | (k != h))
            def _():
                g_move(side, k).start()

        if sweep + 1 < ITERS:
            peak[...] = jnp.full_like(peak, NEGATIVE)
            total[...] = jnp.zeros_like(total)

        @pl.loop(0, 2 * n)
        def _(e):
            side = e // n
            slot = (h + e) % n
            index = side * n + slot

            @pl.when((side == 1) | (slot != h))
            def _():
                pltpu.make_async_copy(
                    gbuf.at[sweep, side, slot], gbuf.at[sweep, side, slot],
                    g_recv.at[sweep, side, slot]).wait()

            g = gbuf[sweep, side, slot] + listed_ref[index]
            if sweep + 1 < ITERS:
                row_update(index, g)
            else:
                chunk = 256
                for r in range(rows // chunk):
                    at = slice(r * chunk, (r + 1) * chunk)
                    f = f_ref[at, :]
                    w = jnp.exp2(
                        (inner[index, at, :] + g) + jnp.concatenate([f] * quarters, axis=1)
                    ).astype(jnp.bfloat16)
                    num_ref[at, :] += jnp.dot(w, pts[side, slot], preferred_element_type=jnp.float32)
                    wide = w.astype(jnp.float32)
                    acc = den_ref[at, :]
                    for q in range(quarters):
                        acc = acc + wide[:, q * LANES:(q + 1) * LANES]
                    den_ref[at, :] = acc

        @pl.loop(0, 2 * n)
        def _(e):
            side, k = e // n, e % n

            @pl.when((side == 1) | (k != h))
            def _():
                part_move(side, k).wait_send()
                g_move(side, k).wait_send()

    @pl.loop(0, n)
    def _(slot):
        each_move(slot, finish)


def shards(groups, n, tiles, cell_slot, counts, src_points, tgt_points):
    help_index = lax.axis_index("help")
    src_index = lax.axis_index("src")
    rows, width = src_points.shape
    zs = line_length(n)
    xs = n // zs
    cost_scale = math.sqrt(width)
    scale = math.log2(math.e) / (EPSILON * cost_scale)
    positions = jnp.arange(rows, dtype=jnp.int32)
    source_live = positions < counts[0, 0]
    target_live = positions < counts[0, 1]
    hx = 0.5 * jnp.sum(jnp.square(src_points.astype(jnp.float32)), axis=1)
    hy = 0.5 * jnp.sum(jnp.square(tgt_points.astype(jnp.float32)), axis=1)
    aux = jnp.where(target_live, -scale * hy, NEGATIVE)[None, :]
    src_slot = lookup(tiles[0], cell_slot[0])
    tgt_slot = lookup(tiles[1], cell_slot[1])
    keys = jnp.where(tgt_slot // n == src_index, 0, n) + tgt_slot % n
    mine = src_slot % n == help_index
    listed = jnp.any(mine[:, None] & (keys[:, None] == jnp.arange(2 * n)[None, :]), axis=0)
    listed_bias = jnp.broadcast_to(jnp.where(listed, 0.0, NEGATIVE)[:, None, None], (2 * n, 1, rows))
    slive = jnp.broadcast_to(source_live.astype(jnp.float32)[:, None], (rows, LANES))
    tlive = target_live.astype(jnp.float32)[None, :]
    vmem = pl.BlockSpec(memory_space=pltpu.VMEM)
    hbm = pl.BlockSpec(memory_space=pl.ANY)
    f32 = jnp.float32
    dma = pltpu.SemaphoreType.DMA
    num, den, f, g = pl.pallas_call(
        functools.partial(kernel, groups, n, zs, xs, scale),
        out_shape=(
            jax.ShapeDtypeStruct((rows, width), f32),
            jax.ShapeDtypeStruct((rows, LANES), f32),
            jax.ShapeDtypeStruct((rows, LANES), f32),
            jax.ShapeDtypeStruct((1, rows), f32),
        ),
        in_specs=[vmem, hbm, hbm, vmem, vmem, vmem],
        out_specs=(vmem, vmem, vmem, vmem),
        scratch_shapes=[
            pltpu.VMEM((2, n, rows, width), jnp.bfloat16),
            pltpu.VMEM((2, n, 1, rows), f32),
            pltpu.VMEM((2 * n, rows, rows), f32),
            pltpu.VMEM((rows, LANES), f32),
            pltpu.VMEM((rows, LANES), f32),
            pltpu.VMEM((ITERS, 2, n, 2, rows), f32),
            pltpu.VMEM((ITERS, 2, n, 2, rows), f32),
            pltpu.VMEM((ITERS, 2, n, 1, rows), f32),
            dma((2,)),
            dma((2, n)),
            dma((2, n)),
            dma((2 + xs, n)),
            dma((2 + xs, n)),
            dma((ITERS, 2, n)),
            dma((ITERS, 2, n)),
            dma((ITERS, 2, n)),
            dma((ITERS, 2, n)),
        ],
        compiler_params=pltpu.CompilerParams(
            collective_id=0, has_side_effects=True, vmem_limit_bytes=60 * 1024 * 1024
        ),
    )(src_points, tgt_points, aux, tlive, slive, listed_bias)
    back = EPSILON * math.log(2.0)
    source_own = jnp.where(source_live, back * (f[:, 0] + scale * hx), 0.0)
    target_own = jnp.where(target_live, back * (g[0] + scale * hy), 0.0)
    safe = jnp.where(source_live, jnp.sum(den, axis=1), 1.0)
    transport = jnp.where(source_live[:, None], num / safe[:, None], 0.0)
    return (source_own, target_own, transport)


def solution(mesh):
    in_specs = (
        P(None, "src"),
        P(),
        P(("src", "help"), None),
        P(("src", "help"), None),
        P(("src", "help"), None),
    )
    out_specs = (P(("src", "help")), P(("src", "help")), P(("src", "help"), None))
    body = functools.partial(shards, mesh.shape["src"], mesh.shape["help"])
    return jax.shard_map(body, mesh=mesh, in_specs=in_specs, out_specs=out_specs, check_vma=False)
```

```python
import functools
import math

import jax
import jax.numpy as jnp
from jax import lax
from jax.experimental import pallas as pl
from jax.experimental.pallas import tpu as pltpu
from jax.sharding import PartitionSpec as P

ITERS = 2
EPSILON = 0.2
NEGATIVE = -1e30
LANES = 128
MESH = pl.DeviceIdType.MESH


def line_length(count):
    return 1 << ((count.bit_length()) // 2)


def kernel(
    groups, n, zs, xs, scale,
    tiles_ref, cell_slot_ref, counts_ref, src_ref, tgt_ref,
    source_ref, target_ref, out_ref,
    pts, aux, inner, peak, total, den, f_ref, hx, listed, part, inbox, gbuf,
    local_sem, rp, ra, sp, sa, part_send, part_recv, g_send, g_recv,
):
    s = lax.axis_index("src")
    h = lax.axis_index("help")
    z, x = h // xs, h % xs
    nxt = (s + 1) % groups
    prv = (s + groups - 1) % groups
    rows, width = src_ref.shape
    quarters = rows // LANES

    cp = pltpu.make_async_copy(tgt_ref, pts.at[0, h], local_sem)
    cp.start()

    barrier = pltpu.get_barrier_semaphore()

    @pl.loop(0, n)
    def _(k):
        pl.semaphore_signal(barrier, inc=1, device_id={"src": nxt, "help": k}, device_id_type=MESH)
        pl.semaphore_signal(barrier, inc=1, device_id={"src": prv, "help": k}, device_id_type=MESH)

        @pl.when(k != h)
        def _():
            pl.semaphore_signal(barrier, inc=1, device_id={"src": s, "help": k}, device_id_type=MESH)

    peak[...] = jnp.full_like(peak, NEGATIVE)
    total[...] = jnp.zeros_like(total)
    den[...] = jnp.zeros_like(den)
    out_ref[...] = jnp.zeros_like(out_ref)
    source_count = counts_ref[0, 0]
    target_count = counts_ref[0, 1]
    target_live = lax.broadcasted_iota(jnp.int32, (1, rows), 1) < target_count

    keys = lax.broadcasted_iota(jnp.int32, listed.shape, 0)

    def mark(t, bias):
        source_slot = cell_slot_ref[0, tiles_ref[0, t]]
        target_slot = cell_slot_ref[1, tiles_ref[1, t]]
        key = jnp.where(target_slot // n == s, 0, n) + target_slot % n
        key = jnp.where(source_slot % n == h, key, 2 * n)
        return jnp.where(keys == key, 0.0, bias)

    listed[...] = lax.fori_loop(
        0, tiles_ref.shape[1], mark, jnp.full(listed.shape, NEGATIVE, jnp.float32))

    def listed_row(index):
        row = listed[pl.ds(index, 1), :]
        return jnp.concatenate([row] * quarters, axis=1)

    def half_norms(load):
        squares = 0.0
        for q in range(width // LANES):
            v = load(slice(q * LANES, (q + 1) * LANES)).astype(jnp.float32)
            squares = squares + v * v
        return (0.5 * scale) * jnp.sum(jnp.transpose(squares), axis=0, keepdims=True)

    hx[...] = half_norms(lambda at: src_ref[:, at])

    def row_update(index, g):
        chunk = 32

        @pl.loop(0, rows // chunk, unroll=2)
        def _(r):
            at = pl.ds(pl.multiple_of(r * chunk, chunk), chunk)
            old = peak[at, :]
            vals = [
                inner[index, at, q * LANES:(q + 1) * LANES] + g[:, q * LANES:(q + 1) * LANES]
                for q in range(quarters)
            ]
            new = functools.reduce(jnp.maximum, vals, old)
            acc = total[at, :] * jnp.exp2(old - new)
            for v in vals:
                acc = acc + jnp.exp2(v - new)
            peak[at, :] = new
            total[at, :] = acc

    def row_finish():
        chunk = 64

        @pl.loop(0, rows // chunk)
        def _(r):
            at = pl.ds(pl.multiple_of(r * chunk, chunk), chunk)
            m = jnp.max(peak[at, :], axis=1, keepdims=True)
            t = jnp.sum(total[at, :] * jnp.exp2(peak[at, :] - m), axis=1, keepdims=True)
            f = -(m + jnp.log2(t))
            row_ids = lax.broadcasted_iota(jnp.int32, (chunk, LANES), 0) + r * chunk
            f_ref[at, :] = jnp.where(row_ids < source_count, f, NEGATIVE)

    def block(side, slot):
        index = side * n + slot
        inner[index] = scale * lax.dot_general(
            src_ref[...], pts[side, slot], (((1,), (1,)), ((), ())),
            preferred_element_type=jnp.float32,
        )
        row_update(index, aux[side, slot] + listed_row(index))

    def moves(kind, slot, side, dev):
        return (
            pltpu.make_async_remote_copy(
                src_ref=pts.at[0, slot], dst_ref=pts.at[side, slot],
                send_sem=sp.at[kind, slot], recv_sem=rp.at[side, slot],
                device_id=dev, device_id_type=MESH),
            pltpu.make_async_remote_copy(
                src_ref=aux.at[0, slot], dst_ref=aux.at[side, slot],
                send_sem=sa.at[kind, slot], recv_sem=ra.at[side, slot],
                device_id=dev, device_id_type=MESH),
        )

    def await_cell(side, slot):
        pltpu.make_async_copy(pts.at[side, slot], pts.at[side, slot], rp.at[side, slot]).wait()
        pltpu.make_async_copy(aux.at[side, slot], aux.at[side, slot], ra.at[side, slot]).wait()

    def each_move(slot, act):
        zz, xx = slot // xs, slot % xs
        mine = xx == x

        @pl.when(mine & (zz <= z) & (z + 1 < zs))
        def _():
            act(moves(0, slot, 0, {"src": s, "help": h + xs}))

        @pl.when(mine & (zz >= z) & (z >= 1))
        def _():
            act(moves(1, slot, 0, {"src": s, "help": h - xs}))

        for k in range(1, xs):
            @pl.when(mine)
            def _(k=k):
                act(moves(2 + k, slot, 0, {"src": s, "help": z * xs + (x + k) % xs}))

        act(moves(2, slot, 1, {"src": prv, "help": h}))

    def start(pair):
        for c in pair:
            c.start()

    def finish(pair):
        for c in pair:
            c.wait_send()

    cp.wait()
    aux[0, h] = jnp.where(target_live, -half_norms(lambda at: pts[0, h, :, at]), NEGATIVE)
    pl.semaphore_wait(barrier, 3 * n - 1)

    def entry(e, dist):
        xoff = (e // 2) % xs
        low = e % 2
        far = dist - jnp.where(xoff > 0, 1, 0)
        zz = jnp.where(low == 0, z - far, z + far)
        valid = (far >= 0) & (far < zs) & (zz >= 0) & (zz < zs) & ((far > 0) | (low == 0))
        return valid, jnp.clip(zz, 0, zs - 1) * xs + (x + xoff) % xs

    @pl.loop(0, zs + 3)
    def _(d):
        @pl.loop(0, 2 * xs)
        def _(e):
            valid, slot = entry(e, d)

            @pl.when(valid)
            def _():
                @pl.when(slot != h)
                def _():
                    await_cell(0, slot)

                each_move(slot, start)

        @pl.loop(0, 4 * xs)
        def _(e):
            side = e // (2 * xs)
            valid, slot = entry(e % (2 * xs), d - 2 * side)

            @pl.when(valid)
            def _():
                @pl.when(side == 1)
                def _():
                    await_cell(1, slot)

                block(side, slot)

    def column(index):
        chunk = 64

        def step(r, state):
            m, t = state
            at = pl.ds(pl.multiple_of(r * chunk, chunk), chunk)
            f = f_ref[at, :]
            v = inner[index, at, :] + jnp.concatenate([f] * quarters, axis=1)
            v = v.reshape(chunk // 8, 8, rows)
            new = jnp.maximum(m, jnp.max(v, axis=0))
            t = t * jnp.exp2(m - new) + jnp.sum(jnp.exp2(v - new[None]), axis=0)
            return new, t

        m, t = lax.fori_loop(
            0, rows // chunk, step,
            (jnp.full((8, rows), NEGATIVE, jnp.float32), jnp.zeros((8, rows), jnp.float32)),
        )
        top = jnp.max(m, axis=0, keepdims=True)
        t = jnp.sum(t * jnp.exp2(m - top), axis=0, keepdims=True)
        return top + listed_row(index), t

    for sweep in range(ITERS):
        row_finish()

        def part_move(side, slot):
            return pltpu.make_async_remote_copy(
                src_ref=part.at[sweep, side, slot], dst_ref=inbox.at[sweep, side, h],
                send_sem=part_send.at[sweep, side, slot], recv_sem=part_recv.at[sweep, side, h],
                device_id={"src": jnp.where(side == 0, s, nxt), "help": slot}, device_id_type=MESH)

        def g_move(side, k):
            return pltpu.make_async_remote_copy(
                src_ref=gbuf.at[sweep, 0, h], dst_ref=gbuf.at[sweep, side, h],
                send_sem=g_send.at[sweep, side, k], recv_sem=g_recv.at[sweep, side, h],
                device_id={"src": jnp.where(side == 0, s, prv), "help": k}, device_id_type=MESH)

        @pl.loop(0, 2 * n)
        def _(e):
            side = 1 - e // n
            slot = (h + 1 + e) % n
            top, t = column(side * n + slot)
            part[sweep, side, slot, 0:1, :] = top
            part[sweep, side, slot, 1:2, :] = t

            @pl.when((side == 1) | (slot != h))
            def _():
                part_move(side, slot).start()

        def join(e, state):
            m, t = state
            side, k = e // n, e % n
            m2 = inbox[sweep, side, k, 0:1, :]
            t2 = inbox[sweep, side, k, 1:2, :]
            new = jnp.maximum(m, m2)
            return new, t * jnp.exp2(m - new) + t2 * jnp.exp2(m2 - new)

        @pl.loop(0, 2 * n)
        def _(e):
            side, k = e // n, e % n

            @pl.when((side == 1) | (k != h))
            def _():
                pltpu.make_async_copy(
                    inbox.at[sweep, side, k], inbox.at[sweep, side, k],
                    part_recv.at[sweep, side, k]).wait()

        inbox[sweep, 0, h] = part[sweep, 0, h]
        m, t = lax.fori_loop(
            1, 2 * n, join, (inbox[sweep, 0, 0, 0:1, :], inbox[sweep, 0, 0, 1:2, :]), unroll=True)
        g = jnp.where(target_live, -(m + jnp.log2(t)), NEGATIVE)
        gbuf[sweep, 0, h] = g

        @pl.loop(0, 2 * n)
        def _(e):
            side, k = e // n, e % n

            @pl.when((side == 1) | (k != h))
            def _():
                g_move(side, k).start()

        if sweep + 1 < ITERS:
            peak[...] = jnp.full_like(peak, NEGATIVE)
            total[...] = jnp.zeros_like(total)

        @pl.loop(0, 2 * n)
        def _(e):
            side = e // n
            slot = (h + e) % n
            index = side * n + slot

            @pl.when((side == 1) | (slot != h))
            def _():
                pltpu.make_async_copy(
                    gbuf.at[sweep, side, slot], gbuf.at[sweep, side, slot],
                    g_recv.at[sweep, side, slot]).wait()

            g = gbuf[sweep, side, slot] + listed_row(index)
            if sweep + 1 < ITERS:
                row_update(index, g)
            else:
                chunk = 256
                for r in range(rows // chunk):
                    at = slice(r * chunk, (r + 1) * chunk)
                    f = f_ref[at, :]
                    w = jnp.exp2(
                        (inner[index, at, :] + g) + jnp.concatenate([f] * quarters, axis=1)
                    ).astype(jnp.bfloat16)
                    out_ref[at, :] += jnp.dot(w, pts[side, slot], preferred_element_type=jnp.float32)
                    wide = w.astype(jnp.float32)
                    acc = den[at, :]
                    for q in range(quarters):
                        acc = acc + wide[:, q * LANES:(q + 1) * LANES]
                    den[at, :] = acc

        @pl.loop(0, 2 * n)
        def _(e):
            side, k = e // n, e % n

            @pl.when((side == 1) | (k != h))
            def _():
                part_move(side, k).wait_send()
                g_move(side, k).wait_send()

    @pl.loop(0, n)
    def _(slot):
        each_move(slot, finish)

    back = EPSILON * math.log(2.0)
    source_live = lax.broadcasted_iota(jnp.int32, (1, rows), 1) < source_count
    f_row = jnp.transpose(f_ref[...])[0:1, :]
    source_ref[...] = jnp.where(source_live, back * (f_row + hx[...]), 0.0)
    target_ref[...] = jnp.where(target_live, back * (gbuf[ITERS - 1, 0, h] - aux[0, h]), 0.0)

    @pl.loop(0, rows // 64)
    def _(r):
        at = pl.ds(pl.multiple_of(r * 64, 64), 64)
        live = lax.broadcasted_iota(jnp.int32, (64, 1), 0) + r * 64 < source_count
        safe = jnp.where(live, jnp.sum(den[at, :], axis=1, keepdims=True), 1.0)
        out_ref[at, :] = jnp.where(live, out_ref[at, :] / safe, 0.0)


def shards(groups, n, tiles, cell_slot, counts, src_points, tgt_points):
    rows, width = src_points.shape
    zs = line_length(n)
    xs = n // zs
    scale = math.log2(math.e) / (EPSILON * math.sqrt(width))
    vmem = pl.BlockSpec(memory_space=pltpu.VMEM)
    smem = pl.BlockSpec(memory_space=pltpu.SMEM)
    hbm = pl.BlockSpec(memory_space=pl.ANY)
    f32 = jnp.float32
    dma = pltpu.SemaphoreType.DMA
    source_own, target_own, transport = pl.pallas_call(
        functools.partial(kernel, groups, n, zs, xs, scale),
        out_shape=(
            jax.ShapeDtypeStruct((1, rows), f32),
            jax.ShapeDtypeStruct((1, rows), f32),
            jax.ShapeDtypeStruct((rows, width), f32),
        ),
        in_specs=[smem, smem, smem, vmem, hbm],
        out_specs=(vmem, vmem, vmem),
        scratch_shapes=[
            pltpu.VMEM((2, n, rows, width), jnp.bfloat16),
            pltpu.VMEM((2, n, 1, rows), f32),
            pltpu.VMEM((2 * n, rows, rows), f32),
            pltpu.VMEM((rows, LANES), f32),
            pltpu.VMEM((rows, LANES), f32),
            pltpu.VMEM((rows, LANES), f32),
            pltpu.VMEM((rows, LANES), f32),
            pltpu.VMEM((1, rows), f32),
            pltpu.VMEM((2 * n, LANES), f32),
            pltpu.VMEM((ITERS, 2, n, 2, rows), f32),
            pltpu.VMEM((ITERS, 2, n, 2, rows), f32),
            pltpu.VMEM((ITERS, 2, n, 1, rows), f32),
            dma,
            dma((2, n)),
            dma((2, n)),
            dma((2 + xs, n)),
            dma((2 + xs, n)),
            dma((ITERS, 2, n)),
            dma((ITERS, 2, n)),
            dma((ITERS, 2, n)),
            dma((ITERS, 2, n)),
        ],
        compiler_params=pltpu.CompilerParams(
            collective_id=0, has_side_effects=True, vmem_limit_bytes=60 * 1024 * 1024
        ),
    )(tiles, cell_slot, counts, src_points, tgt_points)
    return (source_own.reshape(rows), target_own.reshape(rows), transport)


def solution(mesh):
    in_specs = (
        P(None, "src"),
        P(),
        P(("src", "help"), None),
        P(("src", "help"), None),
        P(("src", "help"), None),
    )
    out_specs = (P(("src", "help")), P(("src", "help")), P(("src", "help"), None))
    body = functools.partial(shards, mesh.shape["src"], mesh.shape["help"])
    return jax.shard_map(body, mesh=mesh, in_specs=in_specs, out_specs=out_specs, check_vma=False)
```

```python
import functools
import math

import jax
import jax.numpy as jnp
from jax import lax
from jax.experimental import pallas as pl
from jax.experimental.pallas import tpu as pltpu
from jax.sharding import PartitionSpec as P

ITERS = 2
EPSILON = 0.2
NEGATIVE = -1e30
LANES = 128
PIECES = 2
MESH = pl.DeviceIdType.MESH


def line_length(count):
    return 1 << ((count.bit_length()) // 2)


def kernel(
    groups, n, zs, xs, scale,
    tiles_ref, cell_slot_ref, counts_ref, src_ref, tgt_ref,
    source_ref, target_ref, out_ref,
    pts, aux, inner, peak, total, den, f_ref, hx, listed, part, inbox, gbuf,
    local_sem, rp, ra, sp, sa, part_send, part_recv, g_send, g_recv,
):
    s = lax.axis_index("src")
    h = lax.axis_index("help")
    z, x = h // xs, h % xs
    nxt = (s + 1) % groups
    prv = (s + groups - 1) % groups
    rows, width = src_ref.shape
    quarters = rows // LANES

    piece_rows = rows // PIECES

    def local(p):
        return pltpu.make_async_copy(
            tgt_ref.at[pl.ds(p * piece_rows, piece_rows), :], pts.at[0, h, p], local_sem.at[p])

    for p in range(PIECES):
        local(p).start()

    barrier = pltpu.get_barrier_semaphore()

    def greet(**dev):
        pl.semaphore_signal(barrier, inc=1, device_id=dev, device_id_type=MESH)

    greet(src=nxt, help=h)
    greet(src=prv, help=h)
    for k in range(1, xs):
        greet(src=s, help=z * xs + (x + k) % xs)

    @pl.when(z + 1 < zs)
    def _():
        greet(src=s, help=h + xs)

    @pl.when(z >= 1)
    def _():
        greet(src=s, help=h - xs)

    @pl.when((z >= 1) & (z + 1 < zs))
    def _():
        pl.semaphore_wait(barrier, 3 + xs)

    @pl.when((z < 1) | (z + 1 >= zs))
    def _():
        pl.semaphore_wait(barrier, 2 + xs)

    def move(kind, slot, what, side, dev):
        if what is None:
            return pltpu.make_async_remote_copy(
                src_ref=aux.at[0, slot], dst_ref=aux.at[side, slot],
                send_sem=sa.at[kind, slot], recv_sem=ra.at[side, slot],
                device_id=dev, device_id_type=MESH)
        return pltpu.make_async_remote_copy(
            src_ref=pts.at[0, slot, what], dst_ref=pts.at[side, slot, what],
            send_sem=sp.at[kind, slot, what], recv_sem=rp.at[side, slot, what],
            device_id=dev, device_id_type=MESH)

    def await_piece(side, slot, p):
        ref = pts.at[side, slot, p]
        pltpu.make_async_copy(ref, ref, rp.at[side, slot, p]).wait()

    def await_aux(side, slot):
        ref = aux.at[side, slot]
        pltpu.make_async_copy(ref, ref, ra.at[side, slot]).wait()

    def each_move(slot, what, act):
        zz, xx = slot // xs, slot % xs
        mine = xx == x

        @pl.when(mine & (zz <= z) & (z + 1 < zs))
        def _():
            act(move(0, slot, what, 0, {"src": s, "help": h + xs}))

        @pl.when(mine & (zz >= z) & (z >= 1))
        def _():
            act(move(1, slot, what, 0, {"src": s, "help": h - xs}))

        for k in range(1, xs):
            @pl.when(mine)
            def _(k=k):
                act(move(2 + k, slot, what, 0, {"src": s, "help": z * xs + (x + k) % xs}))

        act(move(2, slot, what, 1, {"src": prv, "help": h}))

    def start(copy):
        copy.start()

    def finish(copy):
        copy.wait_send()

    for p in range(PIECES):
        local(p).wait()
        each_move(h, p, start)

    peak[...] = jnp.full_like(peak, NEGATIVE)
    total[...] = jnp.zeros_like(total)
    den[...] = jnp.zeros_like(den)
    out_ref[...] = jnp.zeros_like(out_ref)
    source_count = counts_ref[0, 0]
    target_count = counts_ref[0, 1]
    target_live = lax.broadcasted_iota(jnp.int32, (1, rows), 1) < target_count

    keys = lax.broadcasted_iota(jnp.int32, listed.shape, 0)

    def mark(t, bias):
        source_slot = cell_slot_ref[0, tiles_ref[0, t]]
        target_slot = cell_slot_ref[1, tiles_ref[1, t]]
        key = jnp.where(target_slot // n == s, 0, n) + target_slot % n
        key = jnp.where(source_slot % n == h, key, 2 * n)
        return jnp.where(keys == key, 0.0, bias)

    listed[...] = lax.fori_loop(
        0, tiles_ref.shape[1], mark, jnp.full(listed.shape, NEGATIVE, jnp.float32))

    def listed_row(index):
        row = listed[pl.ds(index, 1), :]
        return jnp.concatenate([row] * quarters, axis=1)

    def half_norms(load):
        squares = 0.0
        for q in range(width // LANES):
            v = load(slice(q * LANES, (q + 1) * LANES)).astype(jnp.float32)
            squares = squares + v * v
        return (0.5 * scale) * jnp.sum(jnp.transpose(squares), axis=0, keepdims=True)

    hx[...] = half_norms(lambda at: src_ref[:, at])

    def row_update(index, g):
        chunk = 32

        for r in range(rows // chunk):
            at = slice(r * chunk, (r + 1) * chunk)
            old = peak[at, :]
            vals = [
                inner[index, at, q * LANES:(q + 1) * LANES] + g[:, q * LANES:(q + 1) * LANES]
                for q in range(quarters)
            ]
            new = functools.reduce(jnp.maximum, vals, old)
            acc = total[at, :] * jnp.exp2(old - new)
            for v in vals:
                acc = acc + jnp.exp2(v - new)
            peak[at, :] = new
            total[at, :] = acc

    def row_finish():
        chunk = 64

        @pl.loop(0, rows // chunk)
        def _(r):
            at = pl.ds(pl.multiple_of(r * chunk, chunk), chunk)
            m = jnp.max(peak[at, :], axis=1, keepdims=True)
            t = jnp.sum(total[at, :] * jnp.exp2(peak[at, :] - m), axis=1, keepdims=True)
            f = -(m + jnp.log2(t))
            row_ids = lax.broadcasted_iota(jnp.int32, (chunk, LANES), 0) + r * chunk
            f_ref[at, :] = jnp.where(row_ids < source_count, f, NEGATIVE)

    def block(side, slot):
        index = side * n + slot
        inner[index] = scale * lax.dot_general(
            src_ref[...], pts[side, slot].reshape(rows, width), (((1,), (1,)), ((), ())),
            preferred_element_type=jnp.float32,
        )
        row_update(index, aux[side, slot] + listed_row(index))

    aux[0, h] = jnp.where(
        target_live, -half_norms(lambda at: pts[0, h, :, :, at].reshape(rows, LANES)), NEGATIVE)
    each_move(h, None, start)

    def entry(e, dist):
        xoff = (e // 2) % xs
        low = e % 2
        far = dist - jnp.where(xoff > 0, 1, 0)
        zz = jnp.where(low == 0, z - far, z + far)
        valid = (far >= 0) & (far < zs) & (zz >= 0) & (zz < zs) & ((far > 0) | (low == 0))
        return valid, jnp.clip(zz, 0, zs - 1) * xs + (x + xoff) % xs

    @pl.loop(0, zs + 3)
    def _(d):
        @pl.loop(0, PIECES * 2 * xs)
        def _(e):
            p = e // (2 * xs)
            valid, slot = entry(e % (2 * xs), d)

            @pl.when(valid & (slot != h))
            def _():
                await_piece(0, slot, p)
                each_move(slot, p, start)

                @pl.when(p == PIECES - 1)
                def _():
                    await_aux(0, slot)
                    each_move(slot, None, start)

        @pl.loop(0, 4 * xs)
        def _(e):
            side = e // (2 * xs)
            valid, slot = entry(e % (2 * xs), d - 2 * side)

            @pl.when(valid)
            def _():
                @pl.when(side == 1)
                def _():
                    for p in range(PIECES):
                        await_piece(1, slot, p)
                    await_aux(1, slot)

                block(side, slot)

    def column(index):
        chunk = 64

        def scores(r):
            at = slice(r * chunk, (r + 1) * chunk)
            f = f_ref[at, :]
            v = inner[index, at, :] + jnp.concatenate([f] * quarters, axis=1)
            return v.reshape(chunk // 8, 8, rows)

        m = jnp.max(scores(0), axis=0)
        for r in range(1, rows // chunk):
            m = jnp.maximum(m, jnp.max(scores(r), axis=0))
        t = jnp.sum(jnp.exp2(scores(0) - m[None]), axis=0)
        for r in range(1, rows // chunk):
            t = t + jnp.sum(jnp.exp2(scores(r) - m[None]), axis=0)
        top = jnp.max(m, axis=0, keepdims=True)
        t = jnp.sum(t * jnp.exp2(m - top), axis=0, keepdims=True)
        return top + listed_row(index), t

    for sweep in range(ITERS):
        row_finish()

        def part_move(side, slot):
            return pltpu.make_async_remote_copy(
                src_ref=part.at[sweep, side, slot], dst_ref=inbox.at[sweep, side, h],
                send_sem=part_send.at[sweep, side, slot], recv_sem=part_recv.at[sweep, side, h],
                device_id={"src": jnp.where(side == 0, s, nxt), "help": slot}, device_id_type=MESH)

        def g_move(side, k):
            return pltpu.make_async_remote_copy(
                src_ref=gbuf.at[sweep, 0, h], dst_ref=gbuf.at[sweep, side, h],
                send_sem=g_send.at[sweep, side, k], recv_sem=g_recv.at[sweep, side, h],
                device_id={"src": jnp.where(side == 0, s, prv), "help": k}, device_id_type=MESH)

        @pl.loop(0, 2 * n)
        def _(e):
            side = 1 - e // n
            slot = (h + 1 + e) % n
            top, t = column(side * n + slot)
            part[sweep, side, slot, 0:1, :] = top
            part[sweep, side, slot, 1:2, :] = t

            @pl.when((side == 1) | (slot != h))
            def _():
                part_move(side, slot).start()

        def join(e, state):
            m, t = state
            side, k = e // n, e % n
            m2 = inbox[sweep, side, k, 0:1, :]
            t2 = inbox[sweep, side, k, 1:2, :]
            new = jnp.maximum(m, m2)
            return new, t * jnp.exp2(m - new) + t2 * jnp.exp2(m2 - new)

        @pl.loop(0, 2 * n)
        def _(e):
            side, k = e // n, e % n

            @pl.when((side == 1) | (k != h))
            def _():
                pltpu.make_async_copy(
                    inbox.at[sweep, side, k], inbox.at[sweep, side, k],
                    part_recv.at[sweep, side, k]).wait()

        inbox[sweep, 0, h] = part[sweep, 0, h]
        m, t = lax.fori_loop(
            1, 2 * n, join, (inbox[sweep, 0, 0, 0:1, :], inbox[sweep, 0, 0, 1:2, :]), unroll=True)
        g = jnp.where(target_live, -(m + jnp.log2(t)), NEGATIVE)
        gbuf[sweep, 0, h] = g

        @pl.loop(0, 2 * n)
        def _(e):
            side, k = e // n, e % n

            @pl.when((side == 1) | (k != h))
            def _():
                g_move(side, k).start()

        if sweep + 1 < ITERS:
            peak[...] = jnp.full_like(peak, NEGATIVE)
            total[...] = jnp.zeros_like(total)

        @pl.loop(0, 2 * n)
        def _(e):
            side = e // n
            slot = (h + e) % n
            index = side * n + slot

            @pl.when((side == 1) | (slot != h))
            def _():
                pltpu.make_async_copy(
                    gbuf.at[sweep, side, slot], gbuf.at[sweep, side, slot],
                    g_recv.at[sweep, side, slot]).wait()

            g = gbuf[sweep, side, slot] + listed_row(index)
            if sweep + 1 < ITERS:
                row_update(index, g)
            else:
                chunk = 256
                for r in range(rows // chunk):
                    at = slice(r * chunk, (r + 1) * chunk)
                    f = f_ref[at, :]
                    w = jnp.exp2(
                        (inner[index, at, :] + g) + jnp.concatenate([f] * quarters, axis=1)
                    ).astype(jnp.bfloat16)
                    out_ref[at, :] += jnp.dot(w, pts[side, slot].reshape(rows, width), preferred_element_type=jnp.float32)
                    wide = w.astype(jnp.float32)
                    acc = den[at, :]
                    for q in range(quarters):
                        acc = acc + wide[:, q * LANES:(q + 1) * LANES]
                    den[at, :] = acc

        @pl.loop(0, 2 * n)
        def _(e):
            side, k = e // n, e % n

            @pl.when((side == 1) | (k != h))
            def _():
                part_move(side, k).wait_send()
                g_move(side, k).wait_send()

    @pl.loop(0, n)
    def _(slot):
        for p in range(PIECES):
            each_move(slot, p, finish)
        each_move(slot, None, finish)

    back = EPSILON * math.log(2.0)
    source_live = lax.broadcasted_iota(jnp.int32, (1, rows), 1) < source_count
    f_row = jnp.transpose(f_ref[...])[0:1, :]
    source_ref[...] = jnp.where(source_live, back * (f_row + hx[...]), 0.0)
    target_ref[...] = jnp.where(target_live, back * (gbuf[ITERS - 1, 0, h] - aux[0, h]), 0.0)

    @pl.loop(0, rows // 64)
    def _(r):
        at = pl.ds(pl.multiple_of(r * 64, 64), 64)
        live = lax.broadcasted_iota(jnp.int32, (64, 1), 0) + r * 64 < source_count
        safe = jnp.where(live, jnp.sum(den[at, :], axis=1, keepdims=True), 1.0)
        out_ref[at, :] = jnp.where(live, out_ref[at, :] / safe, 0.0)


def shards(groups, n, tiles, cell_slot, counts, src_points, tgt_points):
    rows, width = src_points.shape
    zs = line_length(n)
    xs = n // zs
    scale = math.log2(math.e) / (EPSILON * math.sqrt(width))
    vmem = pl.BlockSpec(memory_space=pltpu.VMEM)
    smem = pl.BlockSpec(memory_space=pltpu.SMEM)
    hbm = pl.BlockSpec(memory_space=pl.ANY)
    f32 = jnp.float32
    dma = pltpu.SemaphoreType.DMA
    source_own, target_own, transport = pl.pallas_call(
        functools.partial(kernel, groups, n, zs, xs, scale),
        out_shape=(
            jax.ShapeDtypeStruct((1, rows), f32),
            jax.ShapeDtypeStruct((1, rows), f32),
            jax.ShapeDtypeStruct((rows, width), f32),
        ),
        in_specs=[smem, smem, smem, vmem, hbm],
        out_specs=(vmem, vmem, vmem),
        scratch_shapes=[
            pltpu.VMEM((2, n, PIECES, rows // PIECES, width), jnp.bfloat16),
            pltpu.VMEM((2, n, 1, rows), f32),
            pltpu.VMEM((2 * n, rows, rows), f32),
            pltpu.VMEM((rows, LANES), f32),
            pltpu.VMEM((rows, LANES), f32),
            pltpu.VMEM((rows, LANES), f32),
            pltpu.VMEM((rows, LANES), f32),
            pltpu.VMEM((1, rows), f32),
            pltpu.VMEM((2 * n, LANES), f32),
            pltpu.VMEM((ITERS, 2, n, 2, rows), f32),
            pltpu.VMEM((ITERS, 2, n, 2, rows), f32),
            pltpu.VMEM((ITERS, 2, n, 1, rows), f32),
            dma((PIECES,)),
            dma((2, n, PIECES)),
            dma((2, n)),
            dma((2 + xs, n, PIECES)),
            dma((2 + xs, n)),
            dma((ITERS, 2, n)),
            dma((ITERS, 2, n)),
            dma((ITERS, 2, n)),
            dma((ITERS, 2, n)),
        ],
        compiler_params=pltpu.CompilerParams(
            collective_id=0, has_side_effects=True, vmem_limit_bytes=60 * 1024 * 1024
        ),
    )(tiles, cell_slot, counts, src_points, tgt_points)
    return (source_own.reshape(rows), target_own.reshape(rows), transport)


def solution(mesh):
    in_specs = (
        P(None, "src"),
        P(),
        P(("src", "help"), None),
        P(("src", "help"), None),
        P(("src", "help"), None),
    )
    out_specs = (P(("src", "help")), P(("src", "help")), P(("src", "help"), None))
    body = functools.partial(shards, mesh.shape["src"], mesh.shape["help"])
    return jax.shard_map(body, mesh=mesh, in_specs=in_specs, out_specs=out_specs, check_vma=False)
```

```python
import functools
import math

import jax
import jax.numpy as jnp
from jax import lax
from jax.experimental import pallas as pl
from jax.experimental.pallas import tpu as pltpu
from jax.sharding import PartitionSpec as P

ITERS = 2
EPSILON = 0.2
NEGATIVE = -1e30
LANES = 128
PIECES = 2
MESH = pl.DeviceIdType.MESH


def line_length(count):
    return 1 << ((count.bit_length()) // 2)


def kernel(
    groups, n, zs, xs, scale,
    tiles_ref, cell_slot_ref, counts_ref, src_ref, tgt_ref,
    source_ref, target_ref, out_ref,
    pts, aux, inner, peak, total, den, f_ref, hx, listed, part, inbox, gbuf,
    local_sem, rp, ra, sp, sa, part_send, part_recv, g_send, g_recv,
):
    s = lax.axis_index("src")
    h = lax.axis_index("help")
    z, x = h // xs, h % xs
    nxt = (s + 1) % groups
    prv = (s + groups - 1) % groups
    rows, width = src_ref.shape
    quarters = rows // LANES

    piece_rows = rows // PIECES

    def local(p):
        return pltpu.make_async_copy(
            tgt_ref.at[pl.ds(p * piece_rows, piece_rows), :], pts.at[0, h, p], local_sem.at[p])

    for p in range(PIECES):
        local(p).start()

    barrier = pltpu.get_barrier_semaphore()

    def greet(**dev):
        pl.semaphore_signal(barrier, inc=1, device_id=dev, device_id_type=MESH)

    greet(src=nxt, help=h)
    greet(src=prv, help=h)
    for k in range(1, xs):
        greet(src=s, help=z * xs + (x + k) % xs)

    @pl.when(z + 1 < zs)
    def _():
        greet(src=s, help=h + xs)

    @pl.when(z >= 1)
    def _():
        greet(src=s, help=h - xs)

    @pl.when((z >= 1) & (z + 1 < zs))
    def _():
        pl.semaphore_wait(barrier, 3 + xs)

    @pl.when((z < 1) | (z + 1 >= zs))
    def _():
        pl.semaphore_wait(barrier, 2 + xs)

    def move(kind, slot, what, side, dev):
        if what is None:
            return pltpu.make_async_remote_copy(
                src_ref=aux.at[0, slot], dst_ref=aux.at[side, slot],
                send_sem=sa.at[kind, slot], recv_sem=ra.at[side, slot],
                device_id=dev, device_id_type=MESH)
        return pltpu.make_async_remote_copy(
            src_ref=pts.at[0, slot, what], dst_ref=pts.at[side, slot, what],
            send_sem=sp.at[kind, slot, what], recv_sem=rp.at[side, slot, what],
            device_id=dev, device_id_type=MESH)

    def await_piece(side, slot, p):
        ref = pts.at[side, slot, p]
        pltpu.make_async_copy(ref, ref, rp.at[side, slot, p]).wait()

    def await_aux(side, slot):
        ref = aux.at[side, slot]
        pltpu.make_async_copy(ref, ref, ra.at[side, slot]).wait()

    def each_move(slot, what, act):
        zz, xx = slot // xs, slot % xs
        mine = xx == x

        @pl.when(mine & (zz <= z) & (z + 1 < zs))
        def _():
            act(move(0, slot, what, 0, {"src": s, "help": h + xs}))

        @pl.when(mine & (zz >= z) & (z >= 1))
        def _():
            act(move(1, slot, what, 0, {"src": s, "help": h - xs}))

        for k in range(1, xs):
            @pl.when(mine)
            def _(k=k):
                act(move(2 + k, slot, what, 0, {"src": s, "help": z * xs + (x + k) % xs}))

        act(move(2, slot, what, 1, {"src": prv, "help": h}))

    def start(copy):
        copy.start()

    def finish(copy):
        copy.wait_send()

    for p in range(PIECES):
        local(p).wait()
        each_move(h, p, start)

    peak[...] = jnp.full_like(peak, NEGATIVE)
    total[...] = jnp.zeros_like(total)
    den[...] = jnp.zeros_like(den)
    out_ref[...] = jnp.zeros_like(out_ref)
    source_count = counts_ref[0, 0]
    target_count = counts_ref[0, 1]
    target_live = lax.broadcasted_iota(jnp.int32, (1, rows), 1) < target_count

    keys = lax.broadcasted_iota(jnp.int32, listed.shape, 0)

    def mark(t, bias):
        source_slot = cell_slot_ref[0, tiles_ref[0, t]]
        target_slot = cell_slot_ref[1, tiles_ref[1, t]]
        key = jnp.where(target_slot // n == s, 0, n) + target_slot % n
        key = jnp.where(source_slot % n == h, key, 2 * n)
        return jnp.where(keys == key, 0.0, bias)

    listed[...] = lax.fori_loop(
        0, tiles_ref.shape[1], mark, jnp.full(listed.shape, NEGATIVE, jnp.float32))

    def listed_row(index):
        row = listed[pl.ds(index, 1), :]
        return jnp.concatenate([row] * quarters, axis=1)

    def half_norms(load):
        squares = 0.0
        for q in range(width // LANES):
            v = load(slice(q * LANES, (q + 1) * LANES)).astype(jnp.float32)
            squares = squares + v * v
        return (0.5 * scale) * jnp.sum(jnp.transpose(squares), axis=0, keepdims=True)

    hx[...] = half_norms(lambda at: src_ref[:, at])

    def row_update(index, g):
        chunk = 32

        for r in range(rows // chunk):
            at = slice(r * chunk, (r + 1) * chunk)
            old = peak[at, :]
            vals = [
                inner[index, at, q * LANES:(q + 1) * LANES] + g[:, q * LANES:(q + 1) * LANES]
                for q in range(quarters)
            ]
            new = functools.reduce(jnp.maximum, vals, old)
            acc = total[at, :] * jnp.exp2(old - new)
            for v in vals:
                acc = acc + jnp.exp2(v - new)
            peak[at, :] = new
            total[at, :] = acc

    def row_finish():
        chunk = 64

        @pl.loop(0, rows // chunk)
        def _(r):
            at = pl.ds(pl.multiple_of(r * chunk, chunk), chunk)
            m = jnp.max(peak[at, :], axis=1, keepdims=True)
            t = jnp.sum(total[at, :] * jnp.exp2(peak[at, :] - m), axis=1, keepdims=True)
            f = -(m + jnp.log2(t))
            row_ids = lax.broadcasted_iota(jnp.int32, (chunk, LANES), 0) + r * chunk
            f_ref[at, :] = jnp.where(row_ids < source_count, f, NEGATIVE)

    def block(side, slot):
        index = side * n + slot
        inner[index] = scale * lax.dot_general(
            src_ref[...], pts[side, slot].reshape(rows, width), (((1,), (1,)), ((), ())),
            preferred_element_type=jnp.float32,
        )
        row_update(index, aux[side, slot] + listed_row(index))

    aux[0, h] = jnp.where(
        target_live, -half_norms(lambda at: pts[0, h, :, :, at].reshape(rows, LANES)), NEGATIVE)
    each_move(h, None, start)

    def entry(e, dist):
        xoff = (e // 2) % xs
        low = e % 2
        far = dist - jnp.where(xoff > 0, 1, 0)
        zz = jnp.where(low == 0, z - far, z + far)
        valid = (far >= 0) & (far < zs) & (zz >= 0) & (zz < zs) & ((far > 0) | (low == 0))
        return valid, jnp.clip(zz, 0, zs - 1) * xs + (x + xoff) % xs

    @pl.loop(0, zs + 2)
    def _(d):
        @pl.loop(0, PIECES * 2 * xs)
        def _(e):
            p = e // (2 * xs)
            valid, slot = entry(e % (2 * xs), d)

            @pl.when(valid & (slot != h))
            def _():
                await_piece(0, slot, p)
                each_move(slot, p, start)

                @pl.when(p == PIECES - 1)
                def _():
                    await_aux(0, slot)
                    each_move(slot, None, start)

        @pl.loop(0, 4 * xs)
        def _(e):
            side = e // (2 * xs)
            valid, slot = entry(e % (2 * xs), d - side)

            @pl.when(valid)
            def _():
                @pl.when(side == 1)
                def _():
                    for p in range(PIECES):
                        await_piece(1, slot, p)
                    await_aux(1, slot)

                block(side, slot)

    def column(index):
        chunk = 64

        def scores(r):
            at = slice(r * chunk, (r + 1) * chunk)
            f = f_ref[at, :]
            v = inner[index, at, :] + jnp.concatenate([f] * quarters, axis=1)
            return v.reshape(chunk // 8, 8, rows)

        m = jnp.max(scores(0), axis=0)
        for r in range(1, rows // chunk):
            m = jnp.maximum(m, jnp.max(scores(r), axis=0))
        t = jnp.sum(jnp.exp2(scores(0) - m[None]), axis=0)
        for r in range(1, rows // chunk):
            t = t + jnp.sum(jnp.exp2(scores(r) - m[None]), axis=0)
        top = jnp.max(m, axis=0, keepdims=True)
        t = jnp.sum(t * jnp.exp2(m - top), axis=0, keepdims=True)
        return top + listed_row(index), t

    for sweep in range(ITERS):
        row_finish()

        def part_move(side, slot):
            return pltpu.make_async_remote_copy(
                src_ref=part.at[sweep, side, slot], dst_ref=inbox.at[sweep, side, h],
                send_sem=part_send.at[sweep, side, slot], recv_sem=part_recv.at[sweep, side, h],
                device_id={"src": jnp.where(side == 0, s, nxt), "help": slot}, device_id_type=MESH)

        def g_move(side, k):
            return pltpu.make_async_remote_copy(
                src_ref=gbuf.at[sweep, 0, h], dst_ref=gbuf.at[sweep, side, h],
                send_sem=g_send.at[sweep, side, k], recv_sem=g_recv.at[sweep, side, h],
                device_id={"src": jnp.where(side == 0, s, prv), "help": k}, device_id_type=MESH)

        @pl.loop(0, 2 * n)
        def _(e):
            side = 1 - e // n
            slot = (h + 1 + e) % n
            top, t = column(side * n + slot)
            part[sweep, side, slot, 0:1, :] = top
            part[sweep, side, slot, 1:2, :] = t

            @pl.when((side == 1) | (slot != h))
            def _():
                part_move(side, slot).start()

        def join(e, state):
            m, t = state
            side, k = e // n, e % n
            m2 = inbox[sweep, side, k, 0:1, :]
            t2 = inbox[sweep, side, k, 1:2, :]
            new = jnp.maximum(m, m2)
            return new, t * jnp.exp2(m - new) + t2 * jnp.exp2(m2 - new)

        @pl.loop(0, 2 * n)
        def _(e):
            side, k = e // n, e % n

            @pl.when((side == 1) | (k != h))
            def _():
                pltpu.make_async_copy(
                    inbox.at[sweep, side, k], inbox.at[sweep, side, k],
                    part_recv.at[sweep, side, k]).wait()

        inbox[sweep, 0, h] = part[sweep, 0, h]
        m, t = lax.fori_loop(
            1, 2 * n, join, (inbox[sweep, 0, 0, 0:1, :], inbox[sweep, 0, 0, 1:2, :]), unroll=True)
        g = jnp.where(target_live, -(m + jnp.log2(t)), NEGATIVE)
        gbuf[sweep, 0, h] = g

        @pl.loop(0, 2 * n)
        def _(e):
            side, k = e // n, e % n

            @pl.when((side == 1) | (k != h))
            def _():
                g_move(side, k).start()

        if sweep + 1 < ITERS:
            peak[...] = jnp.full_like(peak, NEGATIVE)
            total[...] = jnp.zeros_like(total)

        @pl.loop(0, 2 * n)
        def _(e):
            side = e // n
            slot = (h + e) % n
            index = side * n + slot

            @pl.when((side == 1) | (slot != h))
            def _():
                pltpu.make_async_copy(
                    gbuf.at[sweep, side, slot], gbuf.at[sweep, side, slot],
                    g_recv.at[sweep, side, slot]).wait()

            g = gbuf[sweep, side, slot] + listed_row(index)
            if sweep + 1 < ITERS:
                row_update(index, g)
            else:
                chunk = 256
                for r in range(rows // chunk):
                    at = slice(r * chunk, (r + 1) * chunk)
                    f = f_ref[at, :]
                    w = jnp.exp2(
                        (inner[index, at, :] + g) + jnp.concatenate([f] * quarters, axis=1)
                    ).astype(jnp.bfloat16)
                    out_ref[at, :] += jnp.dot(w, pts[side, slot].reshape(rows, width), preferred_element_type=jnp.float32)
                    wide = w.astype(jnp.float32)
                    acc = den[at, :]
                    for q in range(quarters):
                        acc = acc + wide[:, q * LANES:(q + 1) * LANES]
                    den[at, :] = acc

        @pl.loop(0, 2 * n)
        def _(e):
            side, k = e // n, e % n

            @pl.when((side == 1) | (k != h))
            def _():
                part_move(side, k).wait_send()
                g_move(side, k).wait_send()

    @pl.loop(0, n)
    def _(slot):
        for p in range(PIECES):
            each_move(slot, p, finish)
        each_move(slot, None, finish)

    back = EPSILON * math.log(2.0)
    source_live = lax.broadcasted_iota(jnp.int32, (1, rows), 1) < source_count
    f_row = jnp.transpose(f_ref[...])[0:1, :]
    source_ref[...] = jnp.where(source_live, back * (f_row + hx[...]), 0.0)
    target_ref[...] = jnp.where(target_live, back * (gbuf[ITERS - 1, 0, h] - aux[0, h]), 0.0)

    @pl.loop(0, rows // 64)
    def _(r):
        at = pl.ds(pl.multiple_of(r * 64, 64), 64)
        live = lax.broadcasted_iota(jnp.int32, (64, 1), 0) + r * 64 < source_count
        safe = jnp.where(live, jnp.sum(den[at, :], axis=1, keepdims=True), 1.0)
        out_ref[at, :] = jnp.where(live, out_ref[at, :] / safe, 0.0)


def shards(groups, n, tiles, cell_slot, counts, src_points, tgt_points):
    rows, width = src_points.shape
    zs = line_length(n)
    xs = n // zs
    scale = math.log2(math.e) / (EPSILON * math.sqrt(width))
    vmem = pl.BlockSpec(memory_space=pltpu.VMEM)
    smem = pl.BlockSpec(memory_space=pltpu.SMEM)
    hbm = pl.BlockSpec(memory_space=pl.ANY)
    f32 = jnp.float32
    dma = pltpu.SemaphoreType.DMA
    source_own, target_own, transport = pl.pallas_call(
        functools.partial(kernel, groups, n, zs, xs, scale),
        out_shape=(
            jax.ShapeDtypeStruct((1, rows), f32),
            jax.ShapeDtypeStruct((1, rows), f32),
            jax.ShapeDtypeStruct((rows, width), f32),
        ),
        in_specs=[smem, smem, smem, vmem, hbm],
        out_specs=(vmem, vmem, vmem),
        scratch_shapes=[
            pltpu.VMEM((2, n, PIECES, rows // PIECES, width), jnp.bfloat16),
            pltpu.VMEM((2, n, 1, rows), f32),
            pltpu.VMEM((2 * n, rows, rows), f32),
            pltpu.VMEM((rows, LANES), f32),
            pltpu.VMEM((rows, LANES), f32),
            pltpu.VMEM((rows, LANES), f32),
            pltpu.VMEM((rows, LANES), f32),
            pltpu.VMEM((1, rows), f32),
            pltpu.VMEM((2 * n, LANES), f32),
            pltpu.VMEM((ITERS, 2, n, 2, rows), f32),
            pltpu.VMEM((ITERS, 2, n, 2, rows), f32),
            pltpu.VMEM((ITERS, 2, n, 1, rows), f32),
            dma((PIECES,)),
            dma((2, n, PIECES)),
            dma((2, n)),
            dma((2 + xs, n, PIECES)),
            dma((2 + xs, n)),
            dma((ITERS, 2, n)),
            dma((ITERS, 2, n)),
            dma((ITERS, 2, n)),
            dma((ITERS, 2, n)),
        ],
        compiler_params=pltpu.CompilerParams(
            collective_id=0, has_side_effects=True, vmem_limit_bytes=60 * 1024 * 1024
        ),
    )(tiles, cell_slot, counts, src_points, tgt_points)
    return (source_own.reshape(rows), target_own.reshape(rows), transport)


def solution(mesh):
    in_specs = (
        P(None, "src"),
        P(),
        P(("src", "help"), None),
        P(("src", "help"), None),
        P(("src", "help"), None),
    )
    out_specs = (P(("src", "help")), P(("src", "help")), P(("src", "help"), None))
    body = functools.partial(shards, mesh.shape["src"], mesh.shape["help"])
    return jax.shard_map(body, mesh=mesh, in_specs=in_specs, out_specs=out_specs, check_vma=False)
```
